32 devices in a mesh: depth: 2 (over core), freq: 16 (over z, y, x).
Axes of the slice: x: 2, y: 2, z: 4, core: 2. Of those that a mesh axis runs over, the one named last changes fastest.
Arguments:
- p_top: bfloat16 [16, 1024, 128], P('freq'), may hold values from -6 to 6
- upgoing: bfloat16 [2, 16, 1024, 128], P('depth', 'freq'), may hold values from -6 to 6
- extrapolator: bfloat16 [2, 16, 2, 1024, 1024], P('depth', 'freq'), may hold values from -0.125 to 0.125
- reflectivity: bfloat16 [2, 1024, 1024], P('depth', 'freq'), may hold values from -0.1875 to 0.1875
Outputs:
- wavefields: bfloat16 [2, 16, 1024, 128], P('depth', 'freq')
- images: float32 [2, 1024, 1024], P('depth', 'freq')
The draws below stay inside these ranges and needn't reach their ends.
All inputs are finite; a program needn't handle non-finite values.
Results may differ from the reference program's by a relative error of at most 0.014.
Values may be sent and summed in bfloat16 or wider, within the bound.
No kernel may reach another device: no remote copies, remote signals or barrier semaphores. Data moves between devices by JAX's collectives and lax.ppermute only.
A program may use at most 64 MiB of HBM per device.

```python
import jax
import jax.numpy as jnp

NX = 1024
SHOTS = 64
LEVELS = 2
FREQS = 16


def strengthened(array, own_key, source, target, shards_of, factor):
    owner, partner = [(jnp.arange(array.shape[dim]) // (array.shape[dim] // shards_of)).reshape([-1 if axis == dim else 1 for axis in range(array.ndim)]) for dim in (source, target)]
    chosen = jax.random.permutation(own_key, shards_of)[partner]
    strong = (owner == chosen) | (owner == (partner + shards_of // 2) % shards_of)
    return jnp.where(strong, factor * array, array)


def shard_levels(rng, shape, pieces, low, high):
    def one(axis_at, shards_of):
        steps = jax.random.uniform(jax.random.fold_in(jax.random.fold_in(rng, 6), axis_at), (shards_of,), jnp.float32, low / len(pieces), high / len(pieces))
        return jnp.repeat(jnp.exp(steps), shape[axis_at] // shards_of).reshape((-1,) + (1,) * (len(shape) - axis_at - 1))

    level = one(*pieces[0])
    for cut in pieces[1:]:
        level = level * one(*cut)
    return level


def gaussian(rng, dims, width, bound, cuts=(), kind=jnp.bfloat16):
    factor_of = shard_levels(rng, dims, cuts, -0.22, 0.18) if cuts else 1.0
    array = jax.random.normal(rng, dims, jnp.float32) * width * factor_of
    return jnp.minimum(jnp.maximum(array, -bound), bound).astype(kind)


def heavy_noise(key, shape, deviation, reach, cuts, heavy, kind=jnp.bfloat16):
    drawn = deviation * jax.random.normal(key, shape, jnp.float32)
    if cuts:
        drawn = drawn * shard_levels(key, shape, cuts, -0.22, 0.18)
    return jnp.clip(strengthened(drawn, jax.random.fold_in(key, 3), *heavy), -reach, reach).astype(kind)


def setup_inputs(seed: int = 0) -> dict:
    keys = jax.random.split(jax.random.key(seed), 5)
    p_top = gaussian(keys[0], (FREQS, NX, 2 * SHOTS), 1.0, 6.0, ((0, 16),))
    upgoing = heavy_noise(keys[1], (LEVELS, FREQS, NX, 2 * SHOTS), 1.0, 6.0, ((0, 2), (1, 16)), (1, 2, 16, 2.0))
    extrapolator = gaussian(keys[2], (LEVELS, FREQS, 2, NX, NX), (2 * NX) ** -0.5, 0.125, ((0, 2), (1, 16)))
    reflectivity = gaussian(keys[3], (LEVELS, NX, NX), NX ** -0.5, 0.1875, ((0, 2), (1, 16)))
    return {"p_top": p_top, "upgoing": upgoing, "extrapolator": extrapolator, "reflectivity": reflectivity}


def extrapolate(weights, diff):
    half = diff.shape[-1] // 2
    real_w = weights[:, 0].astype(jnp.float32)
    imag_w = weights[:, 1].astype(jnp.float32)
    field = diff.astype(jnp.float32)
    first = jnp.einsum('fij,fjs->fis', real_w, field)
    second = jnp.einsum('fij,fjs->fis', imag_w, field)
    real_part = first[..., :half] - second[..., half:]
    imag_part = first[..., half:] + second[..., :half]
    return jnp.concatenate([real_part, imag_part], axis=-1).astype(jnp.bfloat16)


def reference(p_top, upgoing, extrapolator, reflectivity):
    scale = (2.0 * SHOTS * FREQS) ** -0.5
    field = p_top
    outs = []
    pictures = []
    for level in range(LEVELS):
        upper = upgoing[level].astype(jnp.float32)
        refl = reflectivity[level].astype(jnp.float32)
        rq_level = jnp.einsum('ij,fjs->fis', refl, upper)
        picture = jnp.einsum('fis,fjs->ij', upper, field.astype(jnp.float32)) * scale
        pictures.append(picture)
        diff = (field.astype(jnp.float32) - rq_level).astype(jnp.bfloat16)
        field = extrapolate(extrapolator[level], diff)
        outs.append(field)
    return jnp.stack(outs), jnp.stack(pictures)
```

```python
import functools

import jax
import jax.numpy as jnp
from jax import lax
from jax.experimental import pallas as pl
from jax.experimental.pallas import tpu as pltpu
from jax.sharding import PartitionSpec as P


VMEM = pl.BlockSpec(memory_space=pltpu.VMEM)
MIB = 1 << 20


def plane_size(devices):
    size = 1
    while 4 * size * size <= devices:
        size *= 2
    return size


def swap(value, by):
    devices = lax.axis_size("freq")
    return lax.ppermute(value, "freq", [(i, i ^ by) for i in range(devices)])


def route(value, by, rise, sources):
    devices = lax.axis_size("freq")
    pairs = [
        (d * devices + i, (d + rise) * devices + (i ^ by))
        for d in sources
        for i in range(devices)
    ]
    return lax.ppermute(value, ("depth", "freq"), pairs)


def params(limit):
    return pltpu.CompilerParams(vmem_limit_bytes=limit)


def pieces_kernel(line, plane, *refs):
    blocks, ups, outs = refs[:line], refs[line : line + plane], refs[line + plane :]
    rows = jnp.concatenate([b[...] for b in blocks], axis=0)
    for up, out in zip(ups, outs):
        out[...] = jnp.dot(rows, up[...], preferred_element_type=jnp.float32).astype(out.dtype)


def rq_pieces(blocks, ups):
    line, plane = len(blocks), len(ups)
    rows, nx = blocks[0].shape
    cols = ups[0].shape[1]
    tall = line * rows
    out_shape = [jax.ShapeDtypeStruct((tall, cols), jnp.float32)]
    out_shape += [jax.ShapeDtypeStruct((tall, cols), jnp.bfloat16)] * (plane - 1)
    return pl.pallas_call(
        functools.partial(pieces_kernel, line, plane),
        out_shape=out_shape,
        in_specs=[VMEM] * (line + plane),
        out_specs=[VMEM] * plane,
        compiler_params=params(16 * MIB),
        cost_estimate=pl.CostEstimate(
            flops=2 * tall * nx * cols * plane, bytes_accessed=2 * nx * (tall + plane * cols), transcendentals=0
        ),
        name="rq_pieces",
    )(*blocks, *ups)


def advance_kernel(line, plane, *refs):
    field, pieces, weights, out, diff = refs[0], refs[1 : 1 + plane], refs[1 + plane], refs[2 + plane], refs[3 + plane]
    me = lax.axis_index("freq")
    rows = field.shape[0] // (line * plane)
    cols = field.shape[1]
    for z in range(line):
        for q in range(plane):
            at = pl.multiple_of((me ^ (z * plane + q)) * rows, rows)
            rq = pieces[q][z * rows : (z + 1) * rows, :].astype(jnp.float32)
            diff[pl.ds(at, rows), :] = (field[pl.ds(at, rows), :].astype(jnp.float32) - rq).astype(jnp.bfloat16)
    straight = diff[...]
    half = cols // 2
    turned = jnp.concatenate([-straight[:, half:], straight[:, :half]], axis=1)
    out[...] = (
        jnp.dot(weights[0], straight, preferred_element_type=jnp.float32)
        + jnp.dot(weights[1], turned, preferred_element_type=jnp.float32)
    ).astype(jnp.bfloat16)


def advance(field, pieces, weights, line, plane):
    nx, cols = field.shape
    return pl.pallas_call(
        functools.partial(advance_kernel, line, plane),
        out_shape=jax.ShapeDtypeStruct((nx, cols), jnp.bfloat16),
        in_specs=[VMEM] * (2 + plane),
        out_specs=VMEM,
        scratch_shapes=[pltpu.VMEM((nx, cols), jnp.bfloat16)],
        compiler_params=params(24 * MIB),
        cost_estimate=pl.CostEstimate(flops=4 * nx * nx * cols, bytes_accessed=4 * nx * nx, transcendentals=0),
        name="advance",
    )(field, *pieces, weights)


def picture_kernel(line, plane, *refs):
    ups, fields, outs = refs[:plane], refs[plane : 2 * plane], refs[2 * plane :]
    me = lax.axis_index("freq")
    rows = outs[0].shape[0]
    left = jnp.concatenate(
        [
            jnp.concatenate(
                [up[pl.ds(pl.multiple_of((me ^ (z * plane)) * rows, rows), rows), :] for z in range(line)],
                axis=0,
            )
            for up in ups
        ],
        axis=1,
    )
    right = jnp.concatenate([f[...] for f in fields], axis=1)
    total = lax.dot_general(left, right, (((1,), (1,)), ((), ())), preferred_element_type=jnp.float32)
    for z, out in enumerate(outs):
        out[...] = total[z * rows : (z + 1) * rows].astype(out.dtype)


def picture_parts(ups, fields, line):
    plane = len(ups)
    nx, cols = ups[0].shape
    rows = nx // (line * plane)
    out_shape = [jax.ShapeDtypeStruct((rows, nx), jnp.float32)]
    out_shape += [jax.ShapeDtypeStruct((rows, nx), jnp.bfloat16)] * (line - 1)
    return pl.pallas_call(
        functools.partial(picture_kernel, line, plane),
        out_shape=out_shape,
        in_specs=[VMEM] * (2 * plane),
        out_specs=[VMEM] * line,
        compiler_params=params(24 * MIB),
        cost_estimate=pl.CostEstimate(
            flops=2 * line * rows * nx * cols * plane, bytes_accessed=4 * nx * cols * plane, transcendentals=0
        ),
        name="picture_parts",
    )(*ups, *fields)


def local(p_top, upgoing, extrapolator, reflectivity):
    upper = upgoing[0, 0]
    weights = extrapolator[0, 0]
    own_rows = reflectivity[0]
    top_field = p_top[0]
    sections = lax.axis_size("depth")
    devices = lax.axis_size("freq")
    plane = plane_size(devices)
    line = devices // plane
    is_first = lax.axis_index("depth") == 0

    blocks = [own_rows] + [swap(own_rows, z * plane) for z in range(1, line)]
    ups = [upper] + [swap(upper, q) for q in range(1, plane)]
    tops = [top_field] + [route(top_field, q, 0, [0]) for q in range(1, plane)]
    pieces = rq_pieces(blocks, ups)
    pieces = [pieces[0]] + [swap(pieces[q], q) for q in range(1, plane)]

    incoming = top_field
    for step in range(1, sections):
        below = advance(incoming, pieces, weights, line, plane)
        moved = route(below, 0, 1, range(sections - 1))
        incoming = jnp.where(is_first, top_field, moved)
    fields = [incoming]
    for q in range(1, plane):
        moved = route(below, q, 1, range(sections - 1))
        fields.append(jnp.where(is_first, tops[q], moved))
    parts = picture_parts(ups, fields, line)
    total = parts[0]
    for z in range(1, line):
        total = total + swap(parts[z], z * plane).astype(jnp.float32)
    scale = (float(upper.shape[1]) * devices) ** (-0.5)
    below = advance(incoming, pieces, weights, line, plane)
    return (below[None, None], (total * scale)[None])


def solution(mesh):
    in_specs = (
        P("freq", None, None),
        P("depth", "freq", None, None),
        P("depth", "freq", None, None, None),
        P("depth", "freq", None),
    )
    out_specs = (P("depth", "freq", None, None), P("depth", "freq", None))
    return jax.shard_map(local, mesh=mesh, in_specs=in_specs, out_specs=out_specs, check_vma=False)
```

```python
import functools

import jax
import jax.numpy as jnp
from jax import lax
from jax.experimental import pallas as pl
from jax.experimental.pallas import tpu as pltpu
from jax.sharding import PartitionSpec as P


VMEM = pl.BlockSpec(memory_space=pltpu.VMEM)
MIB = 1 << 20


def plane_size(devices):
    size = 1
    while 4 * size * size <= devices:
        size *= 2
    return size


def swap(value, by):
    devices = lax.axis_size("freq")
    return lax.ppermute(value, "freq", [(i, i ^ by) for i in range(devices)])


def lower(value, by):
    levels, devices = lax.axis_size("depth"), lax.axis_size("freq")
    pairs = [
        (d * devices + i, (d + 1) * devices + (i ^ by) if d + 1 < levels else i)
        for d in range(levels)
        for i in range(devices)
    ]
    return lax.ppermute(value, ("depth", "freq"), pairs)


def raise_top(value, by):
    levels, devices = lax.axis_size("depth"), lax.axis_size("freq")
    pairs = [((devices if levels > 1 else 0) + i, i ^ by) for i in range(devices)]
    if levels > 1:
        pairs += [(i, devices + i) for i in range(devices)]
    return lax.ppermute(value, ("depth", "freq"), pairs)


def params(limit):
    return pltpu.CompilerParams(vmem_limit_bytes=limit)


def stage_kernel(count, *refs):
    sources, targets, sems = refs[:count], refs[count : 2 * count], refs[2 * count]
    copies = [pltpu.make_async_copy(a, b, sems.at[k]) for k, (a, b) in enumerate(zip(sources, targets))]
    for copy in copies:
        copy.start()
    for copy in copies:
        copy.wait()


def stage(*arrays):
    count = len(arrays)
    size = sum(a.size * a.dtype.itemsize for a in arrays)
    return pl.pallas_call(
        functools.partial(stage_kernel, count),
        out_shape=[jax.ShapeDtypeStruct(a.shape, a.dtype) for a in arrays],
        in_specs=[pl.BlockSpec(memory_space=pltpu.HBM)] * count,
        out_specs=[VMEM] * count,
        scratch_shapes=[pltpu.SemaphoreType.DMA((count,))],
        compiler_params=params(16 * MIB),
        cost_estimate=pl.CostEstimate(flops=0, bytes_accessed=2 * size, transcendentals=0),
        name="stage_inputs",
    )(*arrays)


def pieces_kernel(line, plane, *refs):
    blocks, ups, outs = refs[:line], refs[line : line + plane], refs[line + plane :]
    rows = jnp.concatenate([b[...] for b in blocks], axis=0)
    for up, out in zip(ups, outs):
        out[...] = jnp.dot(rows, up[...], preferred_element_type=jnp.float32).astype(out.dtype)


def rq_pieces(blocks, ups):
    line, plane = len(blocks), len(ups)
    rows, nx = blocks[0].shape
    cols = ups[0].shape[1]
    tall = line * rows
    out_shape = [jax.ShapeDtypeStruct((tall, cols), jnp.float32)]
    out_shape += [jax.ShapeDtypeStruct((tall, cols), jnp.bfloat16)] * (plane - 1)
    return pl.pallas_call(
        functools.partial(pieces_kernel, line, plane),
        out_shape=out_shape,
        in_specs=[VMEM] * (line + plane),
        out_specs=[VMEM] * plane,
        compiler_params=params(16 * MIB),
        cost_estimate=pl.CostEstimate(
            flops=2 * tall * nx * cols * plane, bytes_accessed=2 * nx * (tall + plane * cols), transcendentals=0
        ),
        name="rq_pieces",
    )(*blocks, *ups)


def advance_kernel(line, plane, *refs):
    top, moved, pieces, weights = refs[0], refs[1], refs[2 : 2 + plane], refs[2 + plane]
    out, diff = refs[-2:]
    me = lax.axis_index("freq")
    first = lax.axis_index("depth") == 0
    rows = top.shape[0] // (line * plane)
    cols = top.shape[1]
    for z in range(line):
        for q in range(plane):
            at = pl.multiple_of((me ^ (z * plane + q)) * rows, rows)
            rq = pieces[q][z * rows : (z + 1) * rows, :].astype(jnp.float32)
            field = jnp.where(first, top[pl.ds(at, rows), :], moved[pl.ds(at, rows), :]).astype(jnp.float32)
            diff[pl.ds(at, rows), :] = (field - rq).astype(jnp.bfloat16)
    straight = diff[...]
    half = cols // 2
    turned = jnp.concatenate([-straight[:, half:], straight[:, :half]], axis=1)
    out[...] = (
        jnp.dot(weights[0], straight, preferred_element_type=jnp.float32)
        + jnp.dot(weights[1], turned, preferred_element_type=jnp.float32)
    ).astype(jnp.bfloat16)


def advance(top, moved, pieces, weights, line, plane):
    nx, cols = top.shape
    return pl.pallas_call(
        functools.partial(advance_kernel, line, plane),
        out_shape=jax.ShapeDtypeStruct((nx, cols), jnp.bfloat16),
        in_specs=[VMEM] * (3 + plane),
        out_specs=VMEM,
        scratch_shapes=[pltpu.VMEM((nx, cols), jnp.bfloat16)],
        compiler_params=params(24 * MIB),
        cost_estimate=pl.CostEstimate(flops=4 * nx * nx * cols, bytes_accessed=4 * nx * nx, transcendentals=0),
        name="advance",
    )(top, moved, *pieces, weights)


def picture_kernel(line, plane, *refs):
    ups, tops, fields, outs = refs[:plane], refs[plane : 2 * plane], refs[2 * plane : 3 * plane], refs[3 * plane :]
    me = lax.axis_index("freq")
    first = lax.axis_index("depth") == 0
    rows = outs[0].shape[0]
    left = jnp.concatenate(
        [
            jnp.concatenate(
                [up[pl.ds(pl.multiple_of((me ^ (z * plane)) * rows, rows), rows), :] for z in range(line)],
                axis=0,
            )
            for up in ups
        ],
        axis=1,
    )
    right = jnp.concatenate([jnp.where(first, t[...], f[...]) for t, f in zip(tops, fields)], axis=1)
    total = lax.dot_general(left, right, (((1,), (1,)), ((), ())), preferred_element_type=jnp.float32)
    for z, out in enumerate(outs):
        out[...] = total[z * rows : (z + 1) * rows].astype(out.dtype)


def picture_parts(ups, tops, fields, line):
    plane = len(ups)
    nx, cols = ups[0].shape
    rows = nx // (line * plane)
    out_shape = [jax.ShapeDtypeStruct((rows, nx), jnp.float32)]
    out_shape += [jax.ShapeDtypeStruct((rows, nx), jnp.bfloat16)] * (line - 1)
    return pl.pallas_call(
        functools.partial(picture_kernel, line, plane),
        out_shape=out_shape,
        in_specs=[VMEM] * (3 * plane),
        out_specs=[VMEM] * line,
        compiler_params=params(24 * MIB),
        cost_estimate=pl.CostEstimate(
            flops=2 * line * rows * nx * cols * plane, bytes_accessed=4 * nx * cols * plane, transcendentals=0
        ),
        name="picture_parts",
    )(*ups, *tops, *fields)


def local(p_top, upgoing, extrapolator, reflectivity):
    return program(p_top[0], upgoing[0, 0], extrapolator[0, 0], reflectivity[0])


def program(top, upper, weights, own_rows):
    sections = lax.axis_size("depth")
    devices = lax.axis_size("freq")
    plane = plane_size(devices)
    line = devices // plane

    blocks = [swap(own_rows, z * plane) for z in range(1, line)]
    ups = [swap(upper, q) for q in range(1, plane)]
    tops = [raise_top(top, q) for q in range(1, plane)]
    top, upper, weights, own_rows = stage(top, upper, weights, own_rows)
    blocks, ups, tops = [own_rows] + blocks, [upper] + ups, [top] + tops
    pieces = rq_pieces(blocks, ups)
    pieces = [pieces[0]] + [swap(pieces[q], q) for q in range(1, plane)]

    moved = top
    for _ in range(1, sections):
        below = advance(top, moved, pieces, weights, line, plane)
        moved = lower(below, 0)
    fields = [moved] + [lower(below, q) for q in range(1, plane)]
    parts = picture_parts(ups, tops, fields, line)
    total = parts[0]
    for z in range(1, line):
        total = total + swap(parts[z], z * plane).astype(jnp.float32)
    scale = (float(upper.shape[1]) * devices) ** (-0.5)
    below = advance(top, moved, pieces, weights, line, plane)
    return (below[None, None], (total * scale)[None])


def solution(mesh):
    in_specs = (
        P("freq", None, None),
        P("depth", "freq", None, None),
        P("depth", "freq", None, None, None),
        P("depth", "freq", None),
    )
    out_specs = (P("depth", "freq", None, None), P("depth", "freq", None))
    return jax.shard_map(local, mesh=mesh, in_specs=in_specs, out_specs=out_specs, check_vma=False)
```

```python
import functools

import jax
import jax.numpy as jnp
from jax import lax
from jax.experimental import pallas as pl
from jax.experimental.pallas import tpu as pltpu
from jax.sharding import PartitionSpec as P


VMEM = pl.BlockSpec(memory_space=pltpu.VMEM)
MIB = 1 << 20
STAGE_LIMIT = 44 * MIB


def plane_size(devices):
    size = 1
    while 4 * size * size <= devices:
        size *= 2
    return size


def swap(value, by):
    devices = lax.axis_size("freq")
    return lax.ppermute(value, "freq", [(i, i ^ by) for i in range(devices)])


def lower(value, by):
    levels, devices = lax.axis_size("depth"), lax.axis_size("freq")
    pairs = [
        (d * devices + i, (d + 1) * devices + (i ^ by) if d + 1 < levels else i)
        for d in range(levels)
        for i in range(devices)
    ]
    return lax.ppermute(value, ("depth", "freq"), pairs)


def raise_top(value, by):
    levels, devices = lax.axis_size("depth"), lax.axis_size("freq")
    pairs = [((devices if levels > 1 else 0) + i, i ^ by) for i in range(devices)]
    if levels > 1:
        pairs += [(i, devices + i) for i in range(devices)]
    return lax.ppermute(value, ("depth", "freq"), pairs)


def reduce_step(value, k, plane, line):
    levels, devices = lax.axis_size("depth"), lax.axis_size("freq")
    pairs = []
    for d in range(levels):
        if k < (line if d else plane):
            by = k * plane if d else k
            pairs += [(d * devices + i, d * devices + (i ^ by)) for i in range(devices)]
    return lax.ppermute(value, ("depth", "freq"), pairs)


def params(limit):
    return pltpu.CompilerParams(vmem_limit_bytes=limit)


def stage_kernel(count, plane, line, *refs):
    sources, other = refs[:count], refs[count]
    targets, loads = refs[count + 1 : 2 * count + 1], refs[2 * count + 1 : -1]
    sems = refs[-1]
    copies = list(zip(sources, targets))
    at_plane = lax.axis_index("freq") // plane
    nx = other.shape[0]
    tall = nx // line
    for z, load in enumerate(loads, 1):
        rows = pl.ds(pl.multiple_of((at_plane ^ z) * tall, tall), tall)
        copies += [(sources[0], load.at[pl.ds(0, nx)]), (other.at[rows], load.at[pl.ds(nx, tall)])]
    copies = [pltpu.make_async_copy(a, b, sems.at[k]) for k, (a, b) in enumerate(copies)]
    for copy in copies:
        copy.start()
    for copy in copies:
        copy.wait()


def stage(arrays, other, plane, line):
    count = len(arrays)
    nx, cols = other.shape
    size = sum(a.size * a.dtype.itemsize for a in arrays)
    out_shape = [jax.ShapeDtypeStruct(a.shape, a.dtype) for a in arrays]
    out_shape += [jax.ShapeDtypeStruct((nx + nx // line, cols), other.dtype)] * (line - 1)
    outs = pl.pallas_call(
        functools.partial(stage_kernel, count, plane, line),
        out_shape=out_shape,
        in_specs=[pl.BlockSpec(memory_space=pl.ANY)] * (count + 1),
        out_specs=[VMEM] * len(out_shape),
        scratch_shapes=[pltpu.SemaphoreType.DMA((count + 2 * (line - 1),))],
        compiler_params=params(STAGE_LIMIT),
        cost_estimate=pl.CostEstimate(flops=0, bytes_accessed=2 * size, transcendentals=0),
        name="stage_inputs",
    )(*arrays, other)
    return outs[:count], outs[count:]


def pieces_kernel(line, plane, *refs):
    blocks, ups, outs = refs[:line], refs[line : line + plane], refs[line + plane :]
    rows = jnp.concatenate([b[...] for b in blocks], axis=0)
    for up, out in zip(ups, outs):
        out[...] = jnp.dot(rows, up[...], preferred_element_type=jnp.float32).astype(out.dtype)


def rq_pieces(blocks, ups):
    line, plane = len(blocks), len(ups)
    rows, nx = blocks[0].shape
    cols = ups[0].shape[1]
    tall = line * rows
    out_shape = [jax.ShapeDtypeStruct((tall, cols), jnp.float32)]
    out_shape += [jax.ShapeDtypeStruct((tall, cols), jnp.bfloat16)] * (plane - 1)
    return pl.pallas_call(
        functools.partial(pieces_kernel, line, plane),
        out_shape=out_shape,
        in_specs=[VMEM] * (line + plane),
        out_specs=[VMEM] * plane,
        compiler_params=params(16 * MIB),
        cost_estimate=pl.CostEstimate(
            flops=2 * tall * nx * cols * plane, bytes_accessed=2 * nx * (tall + plane * cols), transcendentals=0
        ),
        name="rq_pieces",
    )(*blocks, *ups)


def advance_kernel(line, plane, *refs):
    top, moved, pieces, weights = refs[0], refs[1], refs[2 : 2 + plane], refs[2 + plane]
    out, diff = refs[-2:]
    me = lax.axis_index("freq")
    first = lax.axis_index("depth") == 0
    rows = top.shape[0] // (line * plane)
    cols = top.shape[1]
    for z in range(line):
        for q in range(plane):
            at = pl.multiple_of((me ^ (z * plane + q)) * rows, rows)
            rq = pieces[q][z * rows : (z + 1) * rows, :].astype(jnp.float32)
            field = jnp.where(first, top[pl.ds(at, rows), :], moved[pl.ds(at, rows), :]).astype(jnp.float32)
            diff[pl.ds(at, rows), :] = (field - rq).astype(jnp.bfloat16)
    straight = diff[...]
    half = cols // 2
    turned = jnp.concatenate([-straight[:, half:], straight[:, :half]], axis=1)
    out[...] = (
        jnp.dot(weights[0], straight, preferred_element_type=jnp.float32)
        + jnp.dot(weights[1], turned, preferred_element_type=jnp.float32)
    ).astype(jnp.bfloat16)


def advance(top, moved, pieces, weights, line, plane):
    nx, cols = top.shape
    return pl.pallas_call(
        functools.partial(advance_kernel, line, plane),
        out_shape=jax.ShapeDtypeStruct((nx, cols), jnp.bfloat16),
        in_specs=[VMEM] * (3 + plane),
        out_specs=VMEM,
        scratch_shapes=[pltpu.VMEM((nx, cols), jnp.bfloat16)],
        compiler_params=params(24 * MIB),
        cost_estimate=pl.CostEstimate(flops=4 * nx * nx * cols, bytes_accessed=4 * nx * nx, transcendentals=0),
        name="advance",
    )(top, moved, *pieces, weights)


def side_by_side(parts):
    return jnp.concatenate(parts, axis=1)


def stacked_rows(ref, starts, rows):
    return jnp.concatenate([ref[pl.ds(pl.multiple_of(s, rows), rows), :] for s in starts], axis=0)


def picture_kernel(line, plane, *refs):
    ups, fields, refs = refs[:plane], refs[plane : 2 * plane], refs[2 * plane :]
    top, loads, outs = refs[0], refs[1:line], refs[line:]
    me = lax.axis_index("freq")
    first = lax.axis_index("depth") == 0
    nx = top.shape[0]
    rows = outs[0].shape[0]

    def write(left, right, count):
        total = lax.dot_general(left, right, (((1,), (1,)), ((), ())), preferred_element_type=jnp.float32)
        for k, out in enumerate(outs):
            if k < count:
                out[...] = total[k * rows : (k + 1) * rows].astype(out.dtype)

    @pl.when(first)
    def _():
        inner = me % plane
        starts = [(me ^ q) * rows for q in range(plane)]
        lefts = [stacked_rows(ups[0], starts, rows)]
        lefts += [stacked_rows(load, [nx + (inner ^ q) * rows for q in range(plane)], rows) for load in loads]
        rights = [top[...]] + [load[:nx, :] for load in loads]
        write(side_by_side(lefts), side_by_side(rights), plane)

    @pl.when(jnp.logical_not(first))
    def _():
        starts = [(me ^ (z * plane)) * rows for z in range(line)]
        lefts = [stacked_rows(up, starts, rows) for up in ups]
        write(side_by_side(lefts), side_by_side([f[...] for f in fields]), line)


def picture_parts(ups, fields, top, loads, plane, line):
    nx, cols = top.shape
    rows = nx // (line * plane)
    count = max(line, plane)
    out_shape = [jax.ShapeDtypeStruct((rows, nx), jnp.float32)]
    out_shape += [jax.ShapeDtypeStruct((rows, nx), jnp.bfloat16)] * (count - 1)
    return pl.pallas_call(
        functools.partial(picture_kernel, line, plane),
        out_shape=out_shape,
        in_specs=[VMEM] * (2 * plane + line),
        out_specs=[VMEM] * count,
        compiler_params=params(24 * MIB),
        cost_estimate=pl.CostEstimate(
            flops=2 * line * rows * nx * cols * plane, bytes_accessed=4 * nx * cols * plane, transcendentals=0
        ),
        name="picture_parts",
    )(*ups, *fields, top, *loads)


def local(p_top, upgoing, extrapolator, reflectivity):
    return program(p_top[0], upgoing[0, 0], extrapolator[0, 0], reflectivity[0])


def program(top, upper, weights, own_rows):
    sections = lax.axis_size("depth")
    devices = lax.axis_size("freq")
    plane = plane_size(devices)
    line = devices // plane

    other = lower(upper, 0)
    blocks = [swap(own_rows, z * plane) for z in range(1, line)]
    ups = [swap(upper, q) for q in range(1, plane)]
    (top, upper, weights, own_rows), loads = stage((top, upper, weights, own_rows), other, plane, line)
    loads = [raise_top(load, z * plane) for z, load in enumerate(loads, 1)]
    blocks, ups = [own_rows] + blocks, [upper] + ups
    pieces = rq_pieces(blocks, ups)
    pieces = [pieces[0]] + [swap(pieces[q], q) for q in range(1, plane)]

    moved = top
    for _ in range(1, sections):
        below = advance(top, moved, pieces, weights, line, plane)
        moved = lower(below, 0)
    fields = [moved] + [lower(below, q) for q in range(1, plane)]
    parts = picture_parts(ups, fields, top, loads, plane, line)
    total = parts[0]
    for k in range(1, len(parts)):
        total = total + reduce_step(parts[k], k, plane, line).astype(jnp.float32)
    scale = (float(upper.shape[1]) * devices) ** (-0.5)
    below = advance(top, moved, pieces, weights, line, plane)
    return (below[None, None], (total * scale)[None])


def solution(mesh):
    in_specs = (
        P("freq", None, None),
        P("depth", "freq", None, None),
        P("depth", "freq", None, None, None),
        P("depth", "freq", None),
    )
    out_specs = (P("depth", "freq", None, None), P("depth", "freq", None))
    return jax.shard_map(local, mesh=mesh, in_specs=in_specs, out_specs=out_specs, check_vma=False)
```

```python
import functools

import jax
import jax.numpy as jnp
from jax import lax
from jax.experimental import pallas as pl
from jax.experimental.pallas import tpu as pltpu
from jax.sharding import PartitionSpec as P


VMEM = pl.BlockSpec(memory_space=pltpu.VMEM)
MIB = 1 << 20
STAGE_LIMIT = 47 * MIB
HALVES = 1
TWO_STEP = False


def plane_size(devices):
    size = 1
    while 4 * size * size <= devices:
        size *= 2
    return size


def swap(value, by):
    devices = lax.axis_size("freq")
    return lax.ppermute(value, "freq", [(i, i ^ by) for i in range(devices)])


def lower(value, by):
    levels, devices = lax.axis_size("depth"), lax.axis_size("freq")
    pairs = [
        (d * devices + i, (d + 1) * devices + (i ^ by) if d + 1 < levels else i)
        for d in range(levels)
        for i in range(devices)
    ]
    return lax.ppermute(value, ("depth", "freq"), pairs)


def raise_top(value, by):
    levels, devices = lax.axis_size("depth"), lax.axis_size("freq")
    pairs = [((devices if levels > 1 else 0) + i, i ^ by) for i in range(devices)]
    if levels > 1:
        pairs += [(i, devices + i) for i in range(devices)]
    return lax.ppermute(value, ("depth", "freq"), pairs)


def reduce_step(value, k, plane, line):
    levels, devices = lax.axis_size("depth"), lax.axis_size("freq")
    pairs = []
    for d in range(levels):
        if k < (line if d else plane):
            by = k * plane if d else k
            pairs += [(d * devices + i, d * devices + (i ^ by)) for i in range(devices)]
    return lax.ppermute(value, ("depth", "freq"), pairs)


def params(limit):
    return pltpu.CompilerParams(vmem_limit_bytes=limit)


def copy_all(pairs, sems):
    copies = [pltpu.make_async_copy(a, b, sems.at[k]) for k, (a, b) in enumerate(pairs)]
    for copy in copies:
        copy.start()
    for copy in copies:
        copy.wait()


def weights_kernel(source, target, sems):
    tall = source.shape[1] // 2
    parts = [(k, pl.ds(h * tall, tall)) for k in range(2) for h in range(2)]
    copy_all([(source.at[p], target.at[p]) for p in parts], sems)


def stage_weights(weights):
    size = weights.size * weights.dtype.itemsize
    return pl.pallas_call(
        weights_kernel,
        out_shape=jax.ShapeDtypeStruct(weights.shape, weights.dtype),
        in_specs=[pl.BlockSpec(memory_space=pl.ANY)],
        out_specs=VMEM,
        scratch_shapes=[pltpu.SemaphoreType.DMA((4,))],
        compiler_params=params(STAGE_LIMIT),
        cost_estimate=pl.CostEstimate(flops=0, bytes_accessed=2 * size, transcendentals=0),
        name="stage_weights",
    )(weights)


def stage_kernel(count, plane, line, *refs):
    sources, other = refs[:count], refs[count]
    targets, loads = refs[count + 1 : 2 * count + 1], refs[2 * count + 1 : -1]
    copies = list(zip(sources, targets))
    at_plane = lax.axis_index("freq") // plane
    nx = other.shape[0]
    tall = nx // line
    for z, load in enumerate(loads, 1):
        rows = pl.ds(pl.multiple_of((at_plane ^ z) * tall, tall), tall)
        copies += [(sources[0], load.at[pl.ds(0, nx)]), (other.at[rows], load.at[pl.ds(nx, tall)])]
    copy_all(copies, refs[-1])


def stage(arrays, other, plane, line):
    count = len(arrays)
    nx, cols = other.shape
    size = sum(a.size * a.dtype.itemsize for a in arrays) + (line - 1) * (nx + nx // line) * cols * 2
    out_shape = [jax.ShapeDtypeStruct(a.shape, a.dtype) for a in arrays]
    out_shape += [jax.ShapeDtypeStruct((nx + nx // line, cols), other.dtype)] * (line - 1)
    outs = pl.pallas_call(
        functools.partial(stage_kernel, count, plane, line),
        out_shape=out_shape,
        in_specs=[pl.BlockSpec(memory_space=pl.ANY)] * (count + 1),
        out_specs=[VMEM] * len(out_shape),
        scratch_shapes=[pltpu.SemaphoreType.DMA((count + 2 * (line - 1),))],
        compiler_params=params(16 * MIB),
        cost_estimate=pl.CostEstimate(flops=0, bytes_accessed=2 * size, transcendentals=0),
        name="stage_inputs",
    )(*arrays, other)
    return outs[:count], outs[count:]


def pieces_kernel(line, cuts, *refs):
    blocks, refs = refs[:line], refs[line:]
    ups, outs, joined = refs[: sum(cuts)], refs[sum(cuts) : sum(cuts) + len(cuts)], list(refs[sum(cuts) + len(cuts) :])
    rows = jnp.concatenate([b[...] for b in blocks], axis=0)
    for cut, out in zip(cuts, outs):
        parts, ups = ups[:cut], ups[cut:]
        up = parts[0][...] if cut == 1 else jnp.concatenate([p[...] for p in parts], axis=0)
        if cut > 1:
            joined.pop(0)[...] = up
        out[...] = jnp.dot(rows, up, preferred_element_type=jnp.float32).astype(out.dtype)


def rq_pieces(blocks, ups):
    line, plane = len(blocks), len(ups)
    cuts = [len(parts) for parts in ups]
    rows, nx = blocks[0].shape
    cols = ups[0][0].shape[1]
    tall = line * rows
    out_shape = [jax.ShapeDtypeStruct((tall, cols), jnp.float32)]
    out_shape += [jax.ShapeDtypeStruct((tall, cols), jnp.bfloat16)] * (plane - 1)
    out_shape += [jax.ShapeDtypeStruct((nx, cols), jnp.bfloat16)] * sum(cut > 1 for cut in cuts)
    outs = pl.pallas_call(
        functools.partial(pieces_kernel, line, cuts),
        out_shape=out_shape,
        in_specs=[VMEM] * (line + sum(cuts)),
        out_specs=[VMEM] * len(out_shape),
        compiler_params=params(16 * MIB),
        cost_estimate=pl.CostEstimate(
            flops=2 * tall * nx * cols * plane, bytes_accessed=2 * nx * (tall + plane * cols), transcendentals=0
        ),
        name="rq_pieces",
    )(*blocks, *[part for parts in ups for part in parts])
    joined = list(outs[plane:])
    return list(outs[:plane]), [parts[0] if len(parts) == 1 else joined.pop(0) for parts in ups]


def gather_line(value, plane, line):
    found = {0: value}
    for z in range(1, line):
        far = z & (z - 1) if z.bit_count() == 2 else 0
        found[z] = swap(found[far], (z ^ far) * plane)
    return [found[z] for z in range(line)]


def gather_plane(value, plane):
    found = {0: [value]}
    tall = value.shape[0] // 2
    for q in range(1, plane):
        if not TWO_STEP or q.bit_count() != 2:
            found[q] = [swap(value, q)]
    for q in range(1, plane):
        if TWO_STEP and q.bit_count() == 2:
            low, high = q & -q, q & (q - 1)
            found[q] = [swap(found[high][0][:tall], low), swap(found[low][0][tall:], high)]
    return [found[q] for q in range(plane)]


def advance_kernel(line, plane, counts, *refs):
    top, moved, refs = refs[0], refs[1 : 1 + counts[0]], refs[1 + counts[0] :]
    pieces, weights, outs, diff = refs[:plane], refs[plane], refs[plane + 1 : -1], refs[-1]
    me = lax.axis_index("freq")
    first = lax.axis_index("depth") == 0
    rows = top.shape[0] // (line * plane)
    cols = top.shape[1]

    def subtract(field):
        for z in range(line):
            for q in range(plane):
                at = pl.multiple_of((me ^ (z * plane + q)) * rows, rows)
                rq = pieces[q][z * rows : (z + 1) * rows, :].astype(jnp.float32)
                diff[pl.ds(at, rows), :] = (field[pl.ds(at, rows), :].astype(jnp.float32) - rq).astype(jnp.bfloat16)

    @pl.when(first)
    def _():
        subtract(top)

    @pl.when(jnp.logical_not(first))
    def _():
        if not moved:
            diff[...] = jnp.zeros_like(diff)
            return
        tall = top.shape[0] // len(moved)
        for h, part in enumerate(moved):
            diff[h * tall : (h + 1) * tall, :] = part[...]
        subtract(diff)

    straight = diff[...]
    half = cols // 2
    turned = jnp.concatenate([-straight[:, half:], straight[:, :half]], axis=1)
    tall = top.shape[0] // counts[1]
    for h, out in enumerate(outs):
        part = slice(h * tall, (h + 1) * tall)
        out[...] = (
            jnp.dot(weights[0, part, :], straight, preferred_element_type=jnp.float32)
            + jnp.dot(weights[1, part, :], turned, preferred_element_type=jnp.float32)
        ).astype(jnp.bfloat16)


def advance(top, moved, pieces, weights, line, plane, parts):
    nx, cols = top.shape
    return pl.pallas_call(
        functools.partial(advance_kernel, line, plane, (len(moved), parts)),
        out_shape=[jax.ShapeDtypeStruct((nx // parts, cols), jnp.bfloat16)] * parts,
        in_specs=[VMEM] * (2 + len(moved) + plane),
        out_specs=[VMEM] * parts,
        scratch_shapes=[pltpu.VMEM((nx, cols), jnp.bfloat16)],
        compiler_params=params(24 * MIB),
        cost_estimate=pl.CostEstimate(flops=4 * nx * nx * cols, bytes_accessed=4 * nx * nx, transcendentals=0),
        name="advance",
    )(top, *moved, *pieces, weights)


def side_by_side(parts):
    return jnp.concatenate(parts, axis=1)


def stacked_rows(ref, starts, rows):
    return jnp.concatenate([ref[pl.ds(pl.multiple_of(s, rows), rows), :] for s in starts], axis=0)


def picture_kernel(line, plane, part, *refs):
    ups, fields, refs = refs[:plane], refs[plane : 2 * plane], refs[2 * plane :]
    top, loads, outs = refs[0], refs[1:line], refs[line:]
    me = lax.axis_index("freq")
    first = lax.axis_index("depth") == 0
    nx = top.shape[0]
    rows = outs[0].shape[0]

    def write(left, right, count):
        total = lax.dot_general(left, right, (((1,), (1,)), ((), ())), preferred_element_type=jnp.float32)
        for k, out in enumerate(outs):
            if k < count:
                out[...] = total[k * rows : (k + 1) * rows].astype(out.dtype)

    @pl.when(first)
    def _():
        inner = me % plane
        starts = [(me ^ q) * rows for q in range(plane)]
        lefts = [stacked_rows(ups[0], starts, rows)]
        lefts += [stacked_rows(load, [nx + (inner ^ q) * rows for q in range(plane)], rows) for load in loads]
        rights = [top[part, :]] + [load[part, :] for load in loads]
        write(side_by_side(lefts), side_by_side(rights), plane)

    @pl.when(jnp.logical_not(first))
    def _():
        starts = [(me ^ (z * plane)) * rows for z in range(line)]
        lefts = [stacked_rows(up, starts, rows) for up in ups]
        write(side_by_side(lefts), side_by_side([f[...] for f in fields]), line)


def picture_parts(ups, fields, top, loads, plane, line, h):
    nx, cols = top.shape
    rows = nx // (line * plane)
    wide = fields[0].shape[0]
    count = max(line, plane)
    out_shape = [jax.ShapeDtypeStruct((rows, wide), jnp.float32)]
    out_shape += [jax.ShapeDtypeStruct((rows, wide), jnp.bfloat16)] * (count - 1)
    return pl.pallas_call(
        functools.partial(picture_kernel, line, plane, slice(h * wide, (h + 1) * wide)),
        out_shape=out_shape,
        in_specs=[VMEM] * (2 * plane + line),
        out_specs=[VMEM] * count,
        compiler_params=params(24 * MIB),
        cost_estimate=pl.CostEstimate(
            flops=2 * line * rows * wide * cols * plane, bytes_accessed=4 * nx * cols * plane, transcendentals=0
        ),
        name="picture_parts",
    )(*ups, *fields, top, *loads)


def sum_kernel(scale, halves, count, *refs):
    out = refs[-1]
    wide = refs[0].shape[1]
    for h in range(halves):
        part = refs[h * count : (h + 1) * count]
        total = part[0][...]
        for ref in part[1:]:
            total = total + ref[...].astype(jnp.float32)
        out[:, h * wide : (h + 1) * wide] = total * scale


def summed(parts, scale):
    halves, count = len(parts), len(parts[0])
    rows, wide = parts[0][0].shape
    return pl.pallas_call(
        functools.partial(sum_kernel, scale, halves, count),
        out_shape=jax.ShapeDtypeStruct((rows, halves * wide), jnp.float32),
        in_specs=[VMEM] * (halves * count),
        out_specs=VMEM,
        compiler_params=params(8 * MIB),
        cost_estimate=pl.CostEstimate(flops=rows * wide * 8, bytes_accessed=rows * wide * 16, transcendentals=0),
        name="sum_parts",
    )(*[ref for part in parts for ref in part])


def local(p_top, upgoing, extrapolator, reflectivity):
    return program(p_top[0], upgoing[0, 0], extrapolator[0, 0], reflectivity[0])


def program(top, upper, weights, own_rows):
    sections = lax.axis_size("depth")
    devices = lax.axis_size("freq")
    plane = plane_size(devices)
    line = devices // plane

    blocks = gather_line(own_rows, plane, line)
    other = lower(upper, 0)
    ups = gather_plane(upper, plane)
    weights = stage_weights(weights)
    (top, upper, own_rows), loads = stage((top, upper, own_rows), other, plane, line)
    loads = [raise_top(load, z * plane) for z, load in enumerate(loads, 1)]
    blocks, ups = [own_rows] + blocks[1:], [[upper]] + ups[1:]
    pieces, ups = rq_pieces(blocks, ups)
    pieces = [pieces[0]] + [swap(pieces[q], q) for q in range(1, plane)]

    moved = []
    for _ in range(1, sections):
        below = advance(top, moved, pieces, weights, line, plane, HALVES)
        moved = [lower(half, 0) for half in below]
    scale = (float(upper.shape[1]) * devices) ** (-0.5)
    sums = []
    for h in range(HALVES):
        fields = [moved[h]] + [lower(below[h], q) for q in range(1, plane)]
        parts = picture_parts(ups, fields, top, loads, plane, line, h)
        sums.append([parts[0]] + [reduce_step(parts[k], k, plane, line) for k in range(1, len(parts))])
    (below,) = advance(top, moved, pieces, weights, line, plane, 1)
    return (below[None, None], summed(sums, scale)[None])


def solution(mesh):
    in_specs = (
        P("freq", None, None),
        P("depth", "freq", None, None),
        P("depth", "freq", None, None, None),
        P("depth", "freq", None),
    )
    out_specs = (P("depth", "freq", None, None), P("depth", "freq", None))
    return jax.shard_map(local, mesh=mesh, in_specs=in_specs, out_specs=out_specs, check_vma=False)
```

```python
import functools

import jax
import jax.numpy as jnp
from jax import lax
from jax.experimental import pallas as pl
from jax.experimental.pallas import tpu as pltpu
from jax.sharding import PartitionSpec as P


VMEM = pl.BlockSpec(memory_space=pltpu.VMEM)
MIB = 1 << 20
STAGE_LIMIT = 47 * MIB
HALVES = 2
JOINED = (1,)
TWO_STEP = False


def plane_size(devices):
    size = 1
    while 4 * size * size <= devices:
        size *= 2
    return size


def swap(value, by):
    devices = lax.axis_size("freq")
    return lax.ppermute(value, "freq", [(i, i ^ by) for i in range(devices)])


def lower(value, by):
    levels, devices = lax.axis_size("depth"), lax.axis_size("freq")
    pairs = [
        (d * devices + i, (d + 1) * devices + (i ^ by) if d + 1 < levels else i)
        for d in range(levels)
        for i in range(devices)
    ]
    return lax.ppermute(value, ("depth", "freq"), pairs)


def raise_top(value, by):
    levels, devices = lax.axis_size("depth"), lax.axis_size("freq")
    pairs = [((devices if levels > 1 else 0) + i, i ^ by) for i in range(devices)]
    if levels > 1:
        pairs += [(i, devices + i) for i in range(devices)]
    return lax.ppermute(value, ("depth", "freq"), pairs)


def reduce_step(value, k, plane, line):
    levels, devices = lax.axis_size("depth"), lax.axis_size("freq")
    pairs = []
    for d in range(levels):
        if k < (line if d else plane):
            by = k * plane if d else k
            pairs += [(d * devices + i, d * devices + (i ^ by)) for i in range(devices)]
    return lax.ppermute(value, ("depth", "freq"), pairs)


def params(limit):
    return pltpu.CompilerParams(vmem_limit_bytes=limit)


def copy_all(pairs, sems):
    copies = [pltpu.make_async_copy(a, b, sems.at[k]) for k, (a, b) in enumerate(pairs)]
    for copy in copies:
        copy.start()
    for copy in copies:
        copy.wait()


def weights_kernel(source, target, sems):
    tall = source.shape[1] // 2
    parts = [(k, pl.ds(h * tall, tall)) for k in range(2) for h in range(2)]
    copy_all([(source.at[p], target.at[p]) for p in parts], sems)


def stage_weights(weights):
    size = weights.size * weights.dtype.itemsize
    return pl.pallas_call(
        weights_kernel,
        out_shape=jax.ShapeDtypeStruct(weights.shape, weights.dtype),
        in_specs=[pl.BlockSpec(memory_space=pl.ANY)],
        out_specs=VMEM,
        scratch_shapes=[pltpu.SemaphoreType.DMA((4,))],
        compiler_params=params(STAGE_LIMIT),
        cost_estimate=pl.CostEstimate(flops=0, bytes_accessed=2 * size, transcendentals=0),
        name="stage_weights",
    )(weights)


def stage_kernel(count, plane, line, *refs):
    sources, other = refs[:count], refs[count]
    targets, loads = refs[count + 1 : 2 * count + 1], refs[2 * count + 1 : -1]
    copies = list(zip(sources, targets))
    at_plane = lax.axis_index("freq") // plane
    nx = other.shape[0]
    tall = nx // line
    for z, load in enumerate(loads, 1):
        rows = pl.ds(pl.multiple_of((at_plane ^ z) * tall, tall), tall)
        copies += [(sources[0], load.at[pl.ds(0, nx)]), (other.at[rows], load.at[pl.ds(nx, tall)])]
    copy_all(copies, refs[-1])


def stage(arrays, other, plane, line):
    count = len(arrays)
    nx, cols = other.shape
    size = sum(a.size * a.dtype.itemsize for a in arrays) + (line - 1) * (nx + nx // line) * cols * 2
    out_shape = [jax.ShapeDtypeStruct(a.shape, a.dtype) for a in arrays]
    out_shape += [jax.ShapeDtypeStruct((nx + nx // line, cols), other.dtype)] * (line - 1)
    outs = pl.pallas_call(
        functools.partial(stage_kernel, count, plane, line),
        out_shape=out_shape,
        in_specs=[pl.BlockSpec(memory_space=pl.ANY)] * (count + 1),
        out_specs=[VMEM] * len(out_shape),
        scratch_shapes=[pltpu.SemaphoreType.DMA((count + 2 * (line - 1),))],
        compiler_params=params(16 * MIB),
        cost_estimate=pl.CostEstimate(flops=0, bytes_accessed=2 * size, transcendentals=0),
        name="stage_inputs",
    )(*arrays, other)
    return outs[:count], outs[count:]


def pieces_kernel(line, cuts, *refs):
    blocks, refs = refs[:line], refs[line:]
    ups, outs, joined = refs[: sum(cuts)], refs[sum(cuts) : sum(cuts) + len(cuts)], list(refs[sum(cuts) + len(cuts) :])
    rows = jnp.concatenate([b[...] for b in blocks], axis=0)
    for cut, out in zip(cuts, outs):
        parts, ups = ups[:cut], ups[cut:]
        up = parts[0][...] if cut == 1 else jnp.concatenate([p[...] for p in parts], axis=0)
        if cut > 1:
            joined.pop(0)[...] = up
        out[...] = jnp.dot(rows, up, preferred_element_type=jnp.float32).astype(out.dtype)


def rq_pieces(blocks, ups):
    line, plane = len(blocks), len(ups)
    cuts = [len(parts) for parts in ups]
    rows, nx = blocks[0].shape
    cols = ups[0][0].shape[1]
    tall = line * rows
    out_shape = [jax.ShapeDtypeStruct((tall, cols), jnp.float32)]
    out_shape += [jax.ShapeDtypeStruct((tall, cols), jnp.bfloat16)] * (plane - 1)
    out_shape += [jax.ShapeDtypeStruct((nx, cols), jnp.bfloat16)] * sum(cut > 1 for cut in cuts)
    outs = pl.pallas_call(
        functools.partial(pieces_kernel, line, cuts),
        out_shape=out_shape,
        in_specs=[VMEM] * (line + sum(cuts)),
        out_specs=[VMEM] * len(out_shape),
        compiler_params=params(16 * MIB),
        cost_estimate=pl.CostEstimate(
            flops=2 * tall * nx * cols * plane, bytes_accessed=2 * nx * (tall + plane * cols), transcendentals=0
        ),
        name="rq_pieces",
    )(*blocks, *[part for parts in ups for part in parts])
    joined = list(outs[plane:])
    return list(outs[:plane]), [parts[0] if len(parts) == 1 else joined.pop(0) for parts in ups]


def gather_line(value, plane, line):
    found = {0: value}
    for z in range(1, line):
        far = z & (z - 1) if z.bit_count() == 2 else 0
        found[z] = swap(found[far], (z ^ far) * plane)
    return [found[z] for z in range(line)]


def gather_plane(value, plane):
    found = {0: [value]}
    tall = value.shape[0] // 2
    for q in range(1, plane):
        if not TWO_STEP or q.bit_count() != 2:
            found[q] = [swap(value, q)]
    for q in range(1, plane):
        if TWO_STEP and q.bit_count() == 2:
            low, high = q & -q, q & (q - 1)
            found[q] = [swap(found[high][0][:tall], low), swap(found[low][0][tall:], high)]
    return [found[q] for q in range(plane)]


def advance_kernel(line, plane, counts, *refs):
    top, moved, refs = refs[0], refs[1 : 1 + counts[0]], refs[1 + counts[0] :]
    pieces, weights, outs, diff = refs[:plane], refs[plane], refs[plane + 1 : -1], refs[-1]
    outs, whole = outs[: counts[1]], outs[-1]
    me = lax.axis_index("freq")
    first = lax.axis_index("depth") == 0
    rows = top.shape[0] // (line * plane)
    cols = top.shape[1]

    def subtract(field):
        for z in range(line):
            for q in range(plane):
                at = pl.multiple_of((me ^ (z * plane + q)) * rows, rows)
                rq = pieces[q][z * rows : (z + 1) * rows, :].astype(jnp.float32)
                diff[pl.ds(at, rows), :] = (field[pl.ds(at, rows), :].astype(jnp.float32) - rq).astype(jnp.bfloat16)

    @pl.when(first)
    def _():
        subtract(top)

    @pl.when(jnp.logical_not(first))
    def _():
        if not moved:
            diff[...] = jnp.zeros_like(diff)
            return
        subtract(moved[0])

    straight = diff[...]
    half = cols // 2
    turned = jnp.concatenate([-straight[:, half:], straight[:, :half]], axis=1)
    tall = top.shape[0] // counts[1]
    for h, out in enumerate(outs):
        part = slice(h * tall, (h + 1) * tall)
        below = (
            jnp.dot(weights[0, part, :], straight, preferred_element_type=jnp.float32)
            + jnp.dot(weights[1, part, :], turned, preferred_element_type=jnp.float32)
        ).astype(jnp.bfloat16)
        out[...] = below
        if counts[1] > 1:
            whole[part, :] = below


def advance(top, moved, pieces, weights, line, plane, parts):
    nx, cols = top.shape
    outs = [jax.ShapeDtypeStruct((nx // parts, cols), jnp.bfloat16)] * parts
    if parts > 1:
        outs.append(jax.ShapeDtypeStruct((nx, cols), jnp.bfloat16))
    return pl.pallas_call(
        functools.partial(advance_kernel, line, plane, (len(moved), parts)),
        out_shape=outs,
        in_specs=[VMEM] * (2 + len(moved) + plane),
        out_specs=[VMEM] * len(outs),
        scratch_shapes=[pltpu.VMEM((nx, cols), jnp.bfloat16)],
        compiler_params=params(24 * MIB),
        cost_estimate=pl.CostEstimate(flops=4 * nx * nx * cols, bytes_accessed=4 * nx * nx, transcendentals=0),
        name="advance",
    )(top, *moved, *pieces, weights)


def side_by_side(parts):
    return jnp.concatenate(parts, axis=1)


def stacked_rows(ref, starts, rows):
    return jnp.concatenate([ref[pl.ds(pl.multiple_of(s, rows), rows), :] for s in starts], axis=0)


def picture_kernel(line, plane, part, joined, *refs):
    ups, fields, refs = refs[:plane], refs[plane : 2 * plane], refs[2 * plane :]
    top, loads, refs = refs[0], refs[1:line], refs[line:]
    earlier, outs = (refs[: len(joined)], refs[len(joined) :]) if part.start else ((), refs)
    me = lax.axis_index("freq")
    first = lax.axis_index("depth") == 0
    nx = top.shape[0]
    rows = outs[0].shape[0]

    def write(left, right, count):
        total = lax.dot_general(left, right, (((1,), (1,)), ((), ())), preferred_element_type=jnp.float32)
        for k, out in enumerate(outs):
            if k < count:
                out[:, part if k in joined else slice(None)] = total[k * rows : (k + 1) * rows].astype(out.dtype)

    for k, before in zip(joined, earlier):
        outs[k][:, : part.start] = before[...]

    @pl.when(first)
    def _():
        inner = me % plane
        starts = [(me ^ q) * rows for q in range(plane)]
        lefts = [stacked_rows(ups[0], starts, rows)]
        lefts += [stacked_rows(load, [nx + (inner ^ q) * rows for q in range(plane)], rows) for load in loads]
        rights = [top[part, :]] + [load[part, :] for load in loads]
        write(side_by_side(lefts), side_by_side(rights), plane)

    @pl.when(jnp.logical_not(first))
    def _():
        starts = [(me ^ (z * plane)) * rows for z in range(line)]
        lefts = [stacked_rows(up, starts, rows) for up in ups]
        write(side_by_side(lefts), side_by_side([fields[0][part, :]] + [f[...] for f in fields[1:]]), line)


def picture_parts(ups, fields, top, loads, plane, line, h, earlier):
    nx, cols = top.shape
    rows = nx // (line * plane)
    wide = nx // HALVES
    count = max(line, plane)
    out_shape = [jax.ShapeDtypeStruct((rows, wide), jnp.float32)]
    for k in range(1, count):
        out_shape.append(jax.ShapeDtypeStruct((rows, wide * (h + 1) if k in JOINED else wide), jnp.bfloat16))
    before = [earlier[k] for k in JOINED] if h else []
    return pl.pallas_call(
        functools.partial(picture_kernel, line, plane, slice(h * wide, (h + 1) * wide), JOINED),
        out_shape=out_shape,
        in_specs=[VMEM] * (2 * plane + line + len(before)),
        out_specs=[VMEM] * count,
        compiler_params=params(24 * MIB),
        cost_estimate=pl.CostEstimate(
            flops=2 * line * rows * wide * cols * plane, bytes_accessed=4 * nx * cols * plane, transcendentals=0
        ),
        name="picture_parts",
    )(*ups, *fields, top, *loads, *before)


def sum_kernel(scale, counts, *refs):
    joined, refs, out = refs[: counts[0]], refs[counts[0] : -1], refs[-1]
    wide = refs[0].shape[1]
    for h in range(len(refs) // counts[1]):
        part = refs[h * counts[1] : (h + 1) * counts[1]]
        at = slice(h * wide, (h + 1) * wide)
        total = part[0][...]
        for value in [ref[...] for ref in part[1:]] + [ref[:, at] for ref in joined]:
            total = total + value.astype(jnp.float32)
        out[:, at] = total * scale


def summed(joined, parts, scale):
    halves, count = len(parts), len(parts[0])
    rows, wide = parts[0][0].shape
    return pl.pallas_call(
        functools.partial(sum_kernel, scale, (len(joined), count)),
        out_shape=jax.ShapeDtypeStruct((rows, halves * wide), jnp.float32),
        in_specs=[VMEM] * (len(joined) + halves * count),
        out_specs=VMEM,
        compiler_params=params(8 * MIB),
        cost_estimate=pl.CostEstimate(flops=rows * wide * 8, bytes_accessed=rows * wide * 16, transcendentals=0),
        name="sum_parts",
    )(*joined, *[ref for part in parts for ref in part])


def local(p_top, upgoing, extrapolator, reflectivity):
    return program(p_top[0], upgoing[0, 0], extrapolator[0, 0], reflectivity[0])


def program(top, upper, weights, own_rows):
    sections = lax.axis_size("depth")
    devices = lax.axis_size("freq")
    plane = plane_size(devices)
    line = devices // plane

    blocks = gather_line(own_rows, plane, line)
    other = lower(upper, 0)
    ups = gather_plane(upper, plane)
    weights = stage_weights(weights)
    (top, upper, own_rows), loads = stage((top, upper, own_rows), other, plane, line)
    loads = [raise_top(load, z * plane) for z, load in enumerate(loads, 1)]
    blocks, ups = [own_rows] + blocks[1:], [[upper]] + ups[1:]
    pieces, ups = rq_pieces(blocks, ups)
    pieces = [pieces[0]] + [swap(pieces[q], q) for q in range(1, plane)]

    moved = []
    for _ in range(1, sections):
        *halves, below = advance(top, moved, pieces, weights, line, plane, HALVES)
        moved = [lower(below, 0)]
    scale = (float(upper.shape[1]) * devices) ** (-0.5)
    parts, sums = None, []
    for h in range(HALVES):
        fields = moved + [lower(halves[h], q) for q in range(1, plane)]
        parts = picture_parts(ups, fields, top, loads, plane, line, h, parts)
        alone = [k for k in range(1, len(parts)) if k not in JOINED]
        sums.append([parts[0]] + [reduce_step(parts[k], k, plane, line) for k in alone])
    joined = [reduce_step(parts[k], k, plane, line) for k in JOINED]
    (below,) = advance(top, moved, pieces, weights, line, plane, 1)
    return (below[None, None], summed(joined, sums, scale)[None])


def solution(mesh):
    in_specs = (
        P("freq", None, None),
        P("depth", "freq", None, None),
        P("depth", "freq", None, None, None),
        P("depth", "freq", None),
    )
    out_specs = (P("depth", "freq", None, None), P("depth", "freq", None))
    return jax.shard_map(local, mesh=mesh, in_specs=in_specs, out_specs=out_specs, check_vma=False)
```

```python
import functools

import jax
import jax.numpy as jnp
from jax import lax
from jax.experimental import pallas as pl
from jax.experimental.pallas import tpu as pltpu
from jax.sharding import PartitionSpec as P


VMEM = pl.BlockSpec(memory_space=pltpu.VMEM)
MIB = 1 << 20
STAGE_LIMIT = 47 * MIB
HALVES = 2
JOINED = (1,)


def plane_size(devices):
    size = 1
    while 4 * size * size <= devices:
        size *= 2
    return size


def swap(value, by):
    devices = lax.axis_size("freq")
    return lax.ppermute(value, "freq", [(i, i ^ by) for i in range(devices)])


def lower(value, by):
    levels, devices = lax.axis_size("depth"), lax.axis_size("freq")
    pairs = [
        (d * devices + i, (d + 1) * devices + (i ^ by) if d + 1 < levels else i)
        for d in range(levels)
        for i in range(devices)
    ]
    return lax.ppermute(value, ("depth", "freq"), pairs)


def raise_top(value, by):
    levels, devices = lax.axis_size("depth"), lax.axis_size("freq")
    pairs = [((devices if levels > 1 else 0) + i, i ^ by) for i in range(devices)]
    if levels > 1:
        pairs += [(i, devices + i) for i in range(devices)]
    return lax.ppermute(value, ("depth", "freq"), pairs)


def reduce_step(value, k, plane, line):
    levels, devices = lax.axis_size("depth"), lax.axis_size("freq")
    pairs = []
    for d in range(levels):
        if k < (line if d else plane):
            by = k * plane if d else k
            pairs += [(d * devices + i, d * devices + (i ^ by)) for i in range(devices)]
    return lax.ppermute(value, ("depth", "freq"), pairs)


def params(limit):
    return pltpu.CompilerParams(vmem_limit_bytes=limit)


def copy_all(pairs, sems):
    copies = [pltpu.make_async_copy(a, b, sems.at[k]) for k, (a, b) in enumerate(pairs)]
    for copy in copies:
        copy.start()
    for copy in copies:
        copy.wait()


def weights_kernel(source, target, sems):
    tall = source.shape[1] // 2
    parts = [(k, pl.ds(h * tall, tall)) for k in range(2) for h in range(2)]
    copy_all([(source.at[p], target.at[p]) for p in parts], sems)


def stage_weights(weights):
    size = weights.size * weights.dtype.itemsize
    return pl.pallas_call(
        weights_kernel,
        out_shape=jax.ShapeDtypeStruct(weights.shape, weights.dtype),
        in_specs=[pl.BlockSpec(memory_space=pl.ANY)],
        out_specs=VMEM,
        scratch_shapes=[pltpu.SemaphoreType.DMA((4,))],
        compiler_params=params(STAGE_LIMIT),
        cost_estimate=pl.CostEstimate(flops=0, bytes_accessed=2 * size, transcendentals=0),
        name="stage_weights",
    )(weights)


def stage_kernel(count, plane, line, *refs):
    sources, other = refs[:count], refs[count]
    targets, loads = refs[count + 1 : 2 * count + 1], refs[2 * count + 1 : -1]
    copies = list(zip(sources, targets))
    at_plane = lax.axis_index("freq") // plane
    nx = other.shape[0]
    tall = nx // line
    for z, load in enumerate(loads, 1):
        rows = pl.ds(pl.multiple_of((at_plane ^ z) * tall, tall), tall)
        copies += [(sources[0], load.at[pl.ds(0, nx)]), (other.at[rows], load.at[pl.ds(nx, tall)])]
    copy_all(copies, refs[-1])


def stage(arrays, other, plane, line):
    count = len(arrays)
    nx, cols = other.shape
    size = sum(a.size * a.dtype.itemsize for a in arrays) + (line - 1) * (nx + nx // line) * cols * 2
    out_shape = [jax.ShapeDtypeStruct(a.shape, a.dtype) for a in arrays]
    out_shape += [jax.ShapeDtypeStruct((nx + nx // line, cols), other.dtype)] * (line - 1)
    outs = pl.pallas_call(
        functools.partial(stage_kernel, count, plane, line),
        out_shape=out_shape,
        in_specs=[pl.BlockSpec(memory_space=pl.ANY)] * (count + 1),
        out_specs=[VMEM] * len(out_shape),
        scratch_shapes=[pltpu.SemaphoreType.DMA((count + 2 * (line - 1),))],
        compiler_params=params(16 * MIB),
        cost_estimate=pl.CostEstimate(flops=0, bytes_accessed=2 * size, transcendentals=0),
        name="stage_inputs",
    )(*arrays, other)
    return outs[:count], outs[count:]


def side_by_side(parts):
    return jnp.concatenate(parts, axis=1)


def pieces_kernel(line, plane, *refs):
    blocks, ups, outs = refs[:line], refs[line : line + plane], refs[line + plane :]
    rows = jnp.concatenate([b[...] for b in blocks], axis=0)
    cols = ups[0].shape[1]
    products = jnp.dot(rows, side_by_side([up[...] for up in ups]), preferred_element_type=jnp.float32)
    for q, out in enumerate(outs):
        out[...] = products[:, q * cols : (q + 1) * cols].astype(out.dtype)


def rq_pieces(blocks, ups):
    line, plane = len(blocks), len(ups)
    rows, nx = blocks[0].shape
    cols = ups[0].shape[1]
    tall = line * rows
    out_shape = [jax.ShapeDtypeStruct((tall, cols), jnp.float32)]
    out_shape += [jax.ShapeDtypeStruct((tall, cols), jnp.bfloat16)] * (plane - 1)
    return pl.pallas_call(
        functools.partial(pieces_kernel, line, plane),
        out_shape=out_shape,
        in_specs=[VMEM] * (line + plane),
        out_specs=[VMEM] * plane,
        compiler_params=params(16 * MIB),
        cost_estimate=pl.CostEstimate(
            flops=2 * tall * nx * cols * plane, bytes_accessed=2 * nx * (tall + plane * cols), transcendentals=0
        ),
        name="rq_pieces",
    )(*blocks, *ups)


def gather_line(value, plane, line):
    found = {0: value}
    for z in range(1, line):
        far = z & (z - 1) if z.bit_count() == 2 else 0
        found[z] = swap(found[far], (z ^ far) * plane)
    return [found[z] for z in range(line)]


def advance_kernel(line, plane, counts, *refs):
    top, moved, refs = refs[0], refs[1 : 1 + counts[0]], refs[1 + counts[0] :]
    pieces, weights, outs, diff = refs[:plane], refs[plane], refs[plane + 1 : -1], refs[-1]
    outs, whole = outs[: counts[1]], outs[-1]
    me = lax.axis_index("freq")
    first = lax.axis_index("depth") == 0
    rows = top.shape[0] // (line * plane)
    cols = top.shape[1]

    def subtract(field):
        for z in range(line):
            for q in range(plane):
                at = pl.multiple_of((me ^ (z * plane + q)) * rows, rows)
                rq = pieces[q][z * rows : (z + 1) * rows, :].astype(jnp.float32)
                diff[pl.ds(at, rows), :] = (field[pl.ds(at, rows), :].astype(jnp.float32) - rq).astype(jnp.bfloat16)

    @pl.when(first)
    def _():
        subtract(top)

    @pl.when(jnp.logical_not(first))
    def _():
        if not moved:
            diff[...] = jnp.zeros_like(diff)
            return
        subtract(moved[0])

    straight = diff[...]
    half = cols // 2
    turned = jnp.concatenate([-straight[:, half:], straight[:, :half]], axis=1)
    tall = top.shape[0] // counts[1]
    for h, out in enumerate(outs):
        part = slice(h * tall, (h + 1) * tall)
        below = (
            jnp.dot(weights[0, part, :], straight, preferred_element_type=jnp.float32)
            + jnp.dot(weights[1, part, :], turned, preferred_element_type=jnp.float32)
        ).astype(jnp.bfloat16)
        out[...] = below
        if counts[1] > 1:
            whole[part, :] = below


def advance(top, moved, pieces, weights, line, plane, parts):
    nx, cols = top.shape
    outs = [jax.ShapeDtypeStruct((nx // parts, cols), jnp.bfloat16)] * parts
    if parts > 1:
        outs.append(jax.ShapeDtypeStruct((nx, cols), jnp.bfloat16))
    return pl.pallas_call(
        functools.partial(advance_kernel, line, plane, (len(moved), parts)),
        out_shape=outs,
        in_specs=[VMEM] * (2 + len(moved) + plane),
        out_specs=[VMEM] * len(outs),
        scratch_shapes=[pltpu.VMEM((nx, cols), jnp.bfloat16)],
        compiler_params=params(24 * MIB),
        cost_estimate=pl.CostEstimate(flops=4 * nx * nx * cols, bytes_accessed=4 * nx * nx, transcendentals=0),
        name="advance",
    )(top, *moved, *pieces, weights)


def stacked_rows(ref, starts, rows):
    return jnp.concatenate([ref[pl.ds(pl.multiple_of(s, rows), rows), :] for s in starts], axis=0)


def picture_kernel(line, plane, part, joined, *refs):
    ups, fields, refs = refs[:plane], refs[plane : 2 * plane], refs[2 * plane :]
    top, loads, refs = refs[0], refs[1:line], refs[line:]
    earlier, outs = (refs[: len(joined)], refs[len(joined) :]) if part.start else ((), refs)
    me = lax.axis_index("freq")
    first = lax.axis_index("depth") == 0
    nx = top.shape[0]
    rows = outs[0].shape[0]

    def write(left, right, count):
        total = lax.dot_general(left, right, (((1,), (1,)), ((), ())), preferred_element_type=jnp.float32)
        for k, out in enumerate(outs):
            if k < count:
                out[:, part if k in joined else slice(None)] = total[k * rows : (k + 1) * rows].astype(out.dtype)

    for k, before in zip(joined, earlier):
        outs[k][:, : part.start] = before[...]

    @pl.when(first)
    def _():
        inner = me % plane
        starts = [(me ^ q) * rows for q in range(plane)]
        lefts = [stacked_rows(ups[0], starts, rows)]
        lefts += [stacked_rows(load, [nx + (inner ^ q) * rows for q in range(plane)], rows) for load in loads]
        rights = [top[part, :]] + [load[part, :] for load in loads]
        write(side_by_side(lefts), side_by_side(rights), plane)

    @pl.when(jnp.logical_not(first))
    def _():
        starts = [(me ^ (z * plane)) * rows for z in range(line)]
        lefts = [stacked_rows(up, starts, rows) for up in ups]
        write(side_by_side(lefts), side_by_side([fields[0][part, :]] + [f[...] for f in fields[1:]]), line)


def picture_parts(ups, fields, top, loads, plane, line, h, earlier):
    nx, cols = top.shape
    rows = nx // (line * plane)
    wide = nx // HALVES
    count = max(line, plane)
    out_shape = [jax.ShapeDtypeStruct((rows, wide), jnp.float32)]
    for k in range(1, count):
        out_shape.append(jax.ShapeDtypeStruct((rows, wide * (h + 1) if k in JOINED else wide), jnp.bfloat16))
    before = [earlier[k] for k in JOINED] if h else []
    return pl.pallas_call(
        functools.partial(picture_kernel, line, plane, slice(h * wide, (h + 1) * wide), JOINED),
        out_shape=out_shape,
        in_specs=[VMEM] * (2 * plane + line + len(before)),
        out_specs=[VMEM] * count,
        compiler_params=params(24 * MIB),
        cost_estimate=pl.CostEstimate(
            flops=2 * line * rows * wide * cols * plane, bytes_accessed=4 * nx * cols * plane, transcendentals=0
        ),
        name="picture_parts",
    )(*ups, *fields, top, *loads, *before)


def sum_kernel(scale, counts, *refs):
    joined, refs, out = refs[: counts[0]], refs[counts[0] : -1], refs[-1]
    wide = refs[0].shape[1]
    for h in range(len(refs) // counts[1]):
        part = refs[h * counts[1] : (h + 1) * counts[1]]
        at = slice(h * wide, (h + 1) * wide)
        total = part[0][...]
        for value in [ref[...] for ref in part[1:]] + [ref[:, at] for ref in joined]:
            total = total + value.astype(jnp.float32)
        out[:, at] = total * scale


def summed(joined, parts, scale):
    halves, count = len(parts), len(parts[0])
    rows, wide = parts[0][0].shape
    return pl.pallas_call(
        functools.partial(sum_kernel, scale, (len(joined), count)),
        out_shape=jax.ShapeDtypeStruct((rows, halves * wide), jnp.float32),
        in_specs=[VMEM] * (len(joined) + halves * count),
        out_specs=VMEM,
        compiler_params=params(8 * MIB),
        cost_estimate=pl.CostEstimate(flops=rows * wide * 8, bytes_accessed=rows * wide * 16, transcendentals=0),
        name="sum_parts",
    )(*joined, *[ref for part in parts for ref in part])


def local(p_top, upgoing, extrapolator, reflectivity):
    return program(p_top[0], upgoing[0, 0], extrapolator[0, 0], reflectivity[0])


def program(top, upper, weights, own_rows):
    sections = lax.axis_size("depth")
    devices = lax.axis_size("freq")
    plane = plane_size(devices)
    line = devices // plane

    blocks = gather_line(own_rows, plane, line)
    other = lower(upper, 0)
    ups = [upper] + [swap(upper, q) for q in range(1, plane)]
    weights = stage_weights(weights)
    (top, upper, own_rows), loads = stage((top, upper, own_rows), other, plane, line)
    loads = [raise_top(load, z * plane) for z, load in enumerate(loads, 1)]
    blocks, ups = [own_rows] + blocks[1:], [upper] + ups[1:]
    pieces = rq_pieces(blocks, ups)
    pieces = [pieces[0]] + [swap(pieces[q], q) for q in range(1, plane)]

    moved = []
    for _ in range(1, sections):
        *halves, below = advance(top, moved, pieces, weights, line, plane, HALVES)
        moved = [lower(below, 0)]
    scale = (float(upper.shape[1]) * devices) ** (-0.5)
    parts, sums = None, []
    for h in range(HALVES):
        fields = moved + [lower(halves[h], q) for q in range(1, plane)]
        parts = picture_parts(ups, fields, top, loads, plane, line, h, parts)
        alone = [k for k in range(1, len(parts)) if k not in JOINED]
        sums.append([parts[0]] + [reduce_step(parts[k], k, plane, line) for k in alone])
    joined = [reduce_step(parts[k], k, plane, line) for k in JOINED]
    (below,) = advance(top, moved, pieces, weights, line, plane, 1)
    return (below[None, None], summed(joined, sums, scale)[None])


def solution(mesh):
    in_specs = (
        P("freq", None, None),
        P("depth", "freq", None, None),
        P("depth", "freq", None, None, None),
        P("depth", "freq", None),
    )
    out_specs = (P("depth", "freq", None, None), P("depth", "freq", None))
    return jax.shard_map(local, mesh=mesh, in_specs=in_specs, out_specs=out_specs, check_vma=False)
```

```python
import functools

import jax
import jax.numpy as jnp
from jax import lax
from jax.experimental import pallas as pl
from jax.experimental.pallas import tpu as pltpu
from jax.sharding import PartitionSpec as P


VMEM = pl.BlockSpec(memory_space=pltpu.VMEM)
MIB = 1 << 20
STAGE_LIMIT = 47 * MIB
HALVES = 2
JOINED = (1,)


def plane_size(devices):
    size = 1
    while 4 * size * size <= devices:
        size *= 2
    return size


def swap(value, by):
    devices = lax.axis_size("freq")
    return lax.ppermute(value, "freq", [(i, i ^ by) for i in range(devices)])


def lower(value, by):
    levels, devices = lax.axis_size("depth"), lax.axis_size("freq")
    pairs = [
        (d * devices + i, (d + 1) * devices + (i ^ by) if d + 1 < levels else i)
        for d in range(levels)
        for i in range(devices)
    ]
    return lax.ppermute(value, ("depth", "freq"), pairs)


def raise_top(value, by):
    levels, devices = lax.axis_size("depth"), lax.axis_size("freq")
    pairs = [((devices if levels > 1 else 0) + i, i ^ by) for i in range(devices)]
    if levels > 1:
        pairs += [(i, devices + i) for i in range(devices)]
    return lax.ppermute(value, ("depth", "freq"), pairs)


def reduce_step(value, k, plane, line):
    levels, devices = lax.axis_size("depth"), lax.axis_size("freq")
    pairs = []
    for d in range(levels):
        if k < (line if d else plane):
            by = k * plane if d else k
            pairs += [(d * devices + i, d * devices + (i ^ by)) for i in range(devices)]
    return lax.ppermute(value, ("depth", "freq"), pairs)


def params(limit):
    return pltpu.CompilerParams(vmem_limit_bytes=limit)


def copy_all(pairs, sems):
    copies = [pltpu.make_async_copy(a, b, sems.at[k]) for k, (a, b) in enumerate(pairs)]
    for copy in copies:
        copy.start()
    for copy in copies:
        copy.wait()


def weights_kernel(source, target, sems):
    tall = source.shape[1] // 2
    parts = [(k, pl.ds(h * tall, tall)) for k in range(2) for h in range(2)]
    copy_all([(source.at[p], target.at[p]) for p in parts], sems)


def stage_weights(weights):
    size = weights.size * weights.dtype.itemsize
    return pl.pallas_call(
        weights_kernel,
        out_shape=jax.ShapeDtypeStruct(weights.shape, weights.dtype),
        in_specs=[pl.BlockSpec(memory_space=pl.ANY)],
        out_specs=VMEM,
        scratch_shapes=[pltpu.SemaphoreType.DMA((4,))],
        compiler_params=params(STAGE_LIMIT),
        cost_estimate=pl.CostEstimate(flops=0, bytes_accessed=2 * size, transcendentals=0),
        name="stage_weights",
    )(weights)


def stage_kernel(count, plane, line, *refs):
    sources, other = refs[:count], refs[count]
    targets, loads = refs[count + 1 : 2 * count + 1], refs[2 * count + 1 : -1]
    copies = list(zip(sources, targets))
    at_plane = lax.axis_index("freq") // plane
    nx = other.shape[0]
    tall = nx // line
    for z, load in enumerate(loads, 1):
        rows = pl.ds(pl.multiple_of((at_plane ^ z) * tall, tall), tall)
        copies += [(sources[0], load.at[pl.ds(0, nx)]), (other.at[rows], load.at[pl.ds(nx, tall)])]
    copy_all(copies, refs[-1])


def stage(arrays, other, plane, line):
    count = len(arrays)
    nx, cols = other.shape
    size = sum(a.size * a.dtype.itemsize for a in arrays) + (line - 1) * (nx + nx // line) * cols * 2
    out_shape = [jax.ShapeDtypeStruct(a.shape, a.dtype) for a in arrays]
    out_shape += [jax.ShapeDtypeStruct((nx + nx // line, cols), other.dtype)] * (line - 1)
    outs = pl.pallas_call(
        functools.partial(stage_kernel, count, plane, line),
        out_shape=out_shape,
        in_specs=[pl.BlockSpec(memory_space=pl.ANY)] * (count + 1),
        out_specs=[VMEM] * len(out_shape),
        scratch_shapes=[pltpu.SemaphoreType.DMA((count + 2 * (line - 1),))],
        compiler_params=params(16 * MIB),
        cost_estimate=pl.CostEstimate(flops=0, bytes_accessed=2 * size, transcendentals=0),
        name="stage_inputs",
    )(*arrays, other)
    return outs[:count], outs[count:]


def side_by_side(parts):
    return jnp.concatenate(parts, axis=1)


def pieces_kernel(line, plane, *refs):
    blocks, ups, outs = refs[:line], refs[line : line + plane], refs[line + plane :]
    rows = jnp.concatenate([b[...] for b in blocks], axis=0)
    cols = ups[0].shape[1]
    products = jnp.dot(rows, side_by_side([up[...] for up in ups]), preferred_element_type=jnp.float32)
    for q, out in enumerate(outs):
        out[...] = products[:, q * cols : (q + 1) * cols].astype(out.dtype)


def rq_pieces(blocks, ups):
    line, plane = len(blocks), len(ups)
    rows, nx = blocks[0].shape
    cols = ups[0].shape[1]
    tall = line * rows
    out_shape = [jax.ShapeDtypeStruct((tall, cols), jnp.float32)]
    out_shape += [jax.ShapeDtypeStruct((tall, cols), jnp.bfloat16)] * (plane - 1)
    return pl.pallas_call(
        functools.partial(pieces_kernel, line, plane),
        out_shape=out_shape,
        in_specs=[VMEM] * (line + plane),
        out_specs=[VMEM] * plane,
        compiler_params=params(16 * MIB),
        cost_estimate=pl.CostEstimate(
            flops=2 * tall * nx * cols * plane, bytes_accessed=2 * nx * (tall + plane * cols), transcendentals=0
        ),
        name="rq_pieces",
    )(*blocks, *ups)


def gather_line(value, plane, line):
    found = {0: value}
    for z in range(1, line):
        far = z & (z - 1) if z.bit_count() == 2 else 0
        found[z] = swap(found[far], (z ^ far) * plane)
    return [found[z] for z in range(line)]


def advance_kernel(line, plane, counts, *refs):
    top, moved, refs = refs[0], refs[1 : 1 + counts[0]], refs[1 + counts[0] :]
    ready, refs = refs[: counts[2]], refs[counts[2] :]
    pieces, weights, outs, diff = refs[:plane], refs[plane], refs[plane + 1 : -1], refs[-1]
    outs, whole = outs[: counts[1]], outs[-1]
    me = lax.axis_index("freq")
    first = lax.axis_index("depth") == 0
    rows = top.shape[0] // (line * plane)
    cols = top.shape[1]

    def subtract(field):
        for z in range(line):
            for q in range(plane):
                at = pl.multiple_of((me ^ (z * plane + q)) * rows, rows)
                rq = pieces[q][z * rows : (z + 1) * rows, :].astype(jnp.float32)
                diff[pl.ds(at, rows), :] = (field[pl.ds(at, rows), :].astype(jnp.float32) - rq).astype(jnp.bfloat16)

    @pl.when(first)
    def _():
        subtract(top)

    @pl.when(jnp.logical_not(first))
    def _():
        if not moved:
            diff[...] = jnp.zeros_like(diff)
            return
        subtract(moved[0])

    def extrapolate():
        straight = diff[...]
        half = cols // 2
        turned = jnp.concatenate([-straight[:, half:], straight[:, :half]], axis=1)
        tall = top.shape[0] // counts[1]
        for h, out in enumerate(outs):
            part = slice(h * tall, (h + 1) * tall)
            below = (
                jnp.dot(weights[0, part, :], straight, preferred_element_type=jnp.float32)
                + jnp.dot(weights[1, part, :], turned, preferred_element_type=jnp.float32)
            ).astype(jnp.bfloat16)
            out[...] = below
            if counts[1] > 1:
                whole[part, :] = below

    if not ready:
        extrapolate()
        return
    pl.when(jnp.logical_not(first))(extrapolate)

    @pl.when(first)
    def _():
        outs[0][...] = ready[0][...]


def advance(top, moved, ready, pieces, weights, line, plane, parts):
    nx, cols = top.shape
    outs = [jax.ShapeDtypeStruct((nx // parts, cols), jnp.bfloat16)] * parts
    if parts > 1:
        outs.append(jax.ShapeDtypeStruct((nx, cols), jnp.bfloat16))
    return pl.pallas_call(
        functools.partial(advance_kernel, line, plane, (len(moved), parts, len(ready))),
        out_shape=outs,
        in_specs=[VMEM] * (2 + len(moved) + len(ready) + plane),
        out_specs=[VMEM] * len(outs),
        scratch_shapes=[pltpu.VMEM((nx, cols), jnp.bfloat16)],
        compiler_params=params(24 * MIB),
        cost_estimate=pl.CostEstimate(flops=4 * nx * nx * cols, bytes_accessed=4 * nx * nx, transcendentals=0),
        name="advance",
    )(top, *moved, *ready, *pieces, weights)


def stacked_rows(ref, starts, rows):
    return jnp.concatenate([ref[pl.ds(pl.multiple_of(s, rows), rows), :] for s in starts], axis=0)


def picture_kernel(line, plane, part, joined, *refs):
    ups, fields, refs = refs[:plane], refs[plane : 2 * plane], refs[2 * plane :]
    top, loads, refs = refs[0], refs[1:line], refs[line:]
    earlier, outs = (refs[: len(joined)], refs[len(joined) :]) if part.start else ((), refs)
    me = lax.axis_index("freq")
    first = lax.axis_index("depth") == 0
    nx = top.shape[0]
    rows = outs[0].shape[0]

    def write(left, right, count):
        total = lax.dot_general(left, right, (((1,), (1,)), ((), ())), preferred_element_type=jnp.float32)
        for k, out in enumerate(outs):
            if k < count:
                out[:, part if k in joined else slice(None)] = total[k * rows : (k + 1) * rows].astype(out.dtype)

    for k, before in zip(joined, earlier):
        outs[k][:, : part.start] = before[...]

    @pl.when(first)
    def _():
        inner = me % plane
        starts = [(me ^ q) * rows for q in range(plane)]
        lefts = [stacked_rows(ups[0], starts, rows)]
        lefts += [stacked_rows(load, [nx + (inner ^ q) * rows for q in range(plane)], rows) for load in loads]
        rights = [top[part, :]] + [load[part, :] for load in loads]
        write(side_by_side(lefts), side_by_side(rights), plane)

    @pl.when(jnp.logical_not(first))
    def _():
        starts = [(me ^ (z * plane)) * rows for z in range(line)]
        lefts = [stacked_rows(up, starts, rows) for up in ups]
        write(side_by_side(lefts), side_by_side([fields[0][part, :]] + [f[...] for f in fields[1:]]), line)


def picture_parts(ups, fields, top, loads, plane, line, h, earlier):
    nx, cols = top.shape
    rows = nx // (line * plane)
    wide = nx // HALVES
    count = max(line, plane)
    out_shape = [jax.ShapeDtypeStruct((rows, wide), jnp.float32)]
    for k in range(1, count):
        out_shape.append(jax.ShapeDtypeStruct((rows, wide * (h + 1) if k in JOINED else wide), jnp.bfloat16))
    before = [earlier[k] for k in JOINED] if h else []
    return pl.pallas_call(
        functools.partial(picture_kernel, line, plane, slice(h * wide, (h + 1) * wide), JOINED),
        out_shape=out_shape,
        in_specs=[VMEM] * (2 * plane + line + len(before)),
        out_specs=[VMEM] * count,
        compiler_params=params(24 * MIB),
        cost_estimate=pl.CostEstimate(
            flops=2 * line * rows * wide * cols * plane, bytes_accessed=4 * nx * cols * plane, transcendentals=0
        ),
        name="picture_parts",
    )(*ups, *fields, top, *loads, *before)


def sum_kernel(scale, counts, *refs):
    joined, refs, out = refs[: counts[0]], refs[counts[0] : -1], refs[-1]
    wide = refs[0].shape[1]
    for h in range(len(refs) // counts[1]):
        part = refs[h * counts[1] : (h + 1) * counts[1]]
        at = slice(h * wide, (h + 1) * wide)
        total = part[0][...]
        for value in [ref[...] for ref in part[1:]] + [ref[:, at] for ref in joined]:
            total = total + value.astype(jnp.float32)
        out[:, at] = total * scale


def summed(joined, parts, scale):
    halves, count = len(parts), len(parts[0])
    rows, wide = parts[0][0].shape
    return pl.pallas_call(
        functools.partial(sum_kernel, scale, (len(joined), count)),
        out_shape=jax.ShapeDtypeStruct((rows, halves * wide), jnp.float32),
        in_specs=[VMEM] * (len(joined) + halves * count),
        out_specs=VMEM,
        compiler_params=params(8 * MIB),
        cost_estimate=pl.CostEstimate(flops=rows * wide * 8, bytes_accessed=rows * wide * 16, transcendentals=0),
        name="sum_parts",
    )(*joined, *[ref for part in parts for ref in part])


def local(p_top, upgoing, extrapolator, reflectivity):
    return program(p_top[0], upgoing[0, 0], extrapolator[0, 0], reflectivity[0])


def program(top, upper, weights, own_rows):
    sections = lax.axis_size("depth")
    devices = lax.axis_size("freq")
    plane = plane_size(devices)
    line = devices // plane

    blocks = gather_line(own_rows, plane, line)
    other = lower(upper, 0)
    ups = [upper] + [swap(upper, q) for q in range(1, plane)]
    weights = stage_weights(weights)
    (top, upper, own_rows), loads = stage((top, upper, own_rows), other, plane, line)
    loads = [raise_top(load, z * plane) for z, load in enumerate(loads, 1)]
    blocks, ups = [own_rows] + blocks[1:], [upper] + ups[1:]
    pieces = rq_pieces(blocks, ups)
    pieces = [pieces[0]] + [swap(pieces[q], q) for q in range(1, plane)]

    moved = []
    for _ in range(1, sections):
        *halves, below = advance(top, moved, [], pieces, weights, line, plane, HALVES)
        moved = [lower(below, 0)]
    scale = (float(upper.shape[1]) * devices) ** (-0.5)
    parts, sums = None, []
    for h in range(HALVES):
        fields = moved + [lower(halves[h], q) for q in range(1, plane)]
        parts = picture_parts(ups, fields, top, loads, plane, line, h, parts)
        alone = [k for k in range(1, len(parts)) if k not in JOINED]
        sums.append([parts[0]] + [reduce_step(parts[k], k, plane, line) for k in alone])
    joined = [reduce_step(parts[k], k, plane, line) for k in JOINED]
    (below,) = advance(top, moved, [below], pieces, weights, line, plane, 1)
    return (below[None, None], summed(joined, sums, scale)[None])


def solution(mesh):
    in_specs = (
        P("freq", None, None),
        P("depth", "freq", None, None),
        P("depth", "freq", None, None, None),
        P("depth", "freq", None),
    )
    out_specs = (P("depth", "freq", None, None), P("depth", "freq", None))
    return jax.shard_map(local, mesh=mesh, in_specs=in_specs, out_specs=out_specs, check_vma=False)
```
